512 devices in a mesh: ctx: 64 (over y_hi, z, core), dp: 8 (over x, y_lo).
Axes of the slice: x: 4, y: 4 (y_hi: 2, y_lo: 2; y = y_hi * 2 + y_lo), z: 16, core: 2. Of those that a mesh axis runs over, the one named last changes fastest.
Arguments:
- queries: bfloat16 [8192, 2048], P('ctx', 'dp')
- keys: bfloat16 [8192, 2048], P('ctx', 'dp')
- values: bfloat16 [8192, 2048], P('ctx', 'dp'), may hold values from -6 to 6
- old_keys: bfloat16 [2048, 2048], P('ctx', 'dp'), may hold values from -6 to 6
- old_values: bfloat16 [2048, 2048], P('ctx', 'dp'), may hold values from -6 to 6
- conv_keys: bfloat16 [16, 4, 128, 128], P('dp'), may hold values from -0.25 to 0.25
- conv_values: bfloat16 [16, 4, 128, 128], P('dp'), may hold values from -0.25 to 0.25
- out_proj: bfloat16 [4096, 2048], P('ctx', 'dp'), may hold values from -0.125 to 0.125
- residual: bfloat16 [8192, 4096], P('ctx', 'dp'), may hold values from -4 to 4
- gain: bfloat16 [4096], P('dp'), may hold values from 0.5 to 1.5
- span_order: int32 [128], P('ctx'), may hold values from 0 to 127, as said below
- memory_length: int32 [1], replicated, may hold values from 128 to 512
Outputs:
- layer_out: bfloat16 [8192, 4096], P('ctx', 'dp')
The draws below stay inside these ranges and needn't reach their ends.
Inputs may be any that keep to these rules, and one draw needn't show every extreme that they name: `span_order`: entries 2 i and 2 i + 1 are blocks c and 127 - c for some c, in either order; every block appears once. `memory_length`: the valid slots are the last ones.
All inputs are finite; a program needn't handle non-finite values.
Results may differ from the reference program's by a relative error of at most 0.018.
Values may be sent and summed in bfloat16 or wider, within the bound.
A program may use at most 64 MiB of HBM per device.

```python
import math
import jax
import jax.numpy as jnp
from jax import lax

D = 4096
HEAD_DIM = 128
TOK_DEV = 128
HEADS = 16
TOKENS = 8192
SPANS = 128
CMEM = 512
OLD = 2048


def pair_draw(key):
    width = HEADS * HEAD_DIM
    key_k = jax.random.fold_in(key, 101)
    key_q = jax.random.fold_in(key, 102)
    keys_all = jnp.clip(jax.random.normal(key_k, (TOKENS, width), jnp.float32), -6.0, 6.0)
    queries_all = 2.5 * jnp.clip(jax.random.normal(key_q, (TOKENS, width), jnp.float32), -6.0, 6.0)
    return (queries_all, keys_all)


def draw_queries(key, part):
    return pair_draw(key)[0].astype(jnp.bfloat16)


def draw_keys(key, part):
    return pair_draw(key)[1].astype(jnp.bfloat16)


def draw_span_order(key, part):
    half = SPANS // 2
    sigma = jax.random.permutation(jax.random.fold_in(key, 201), half).astype(jnp.int32)
    flip = jax.random.randint(jax.random.fold_in(key, 202), (half,), 0, 2)
    later = (SPANS - 1 - sigma).astype(jnp.int32)
    first = jnp.where(flip == 1, later, sigma)
    second = jnp.where(flip == 1, sigma, later)
    return jnp.stack([first, second], axis=1).reshape(SPANS).astype(jnp.int32)


def levels(rng, dims, shards, low, largest):
    loudness, own = 1.0, jax.random.fold_in(rng, 6)
    for position, blocks in shards:
        draws = jnp.exp(jax.random.uniform(jax.random.fold_in(own, position), (blocks,), jnp.float32, low / len(shards), largest / len(shards)))
        loudness = loudness * jnp.repeat(draws, dims[position] // blocks).reshape([-1 if axis == position else 1 for axis in range(len(dims))])
    return loudness


def gaussian(rng, dims, scale, most, cuts=(), kind=jnp.bfloat16):
    loudness = levels(rng, dims, cuts, -0.22, 0.18) if cuts else 1.0
    values = jax.random.normal(rng, dims, jnp.float32) * scale * loudness
    return jnp.minimum(jnp.maximum(values, -most), most).astype(kind)


def setup_inputs(seed: int = 0) -> dict:
    seeds = jax.random.split(jax.random.key(seed), 13)
    return {
        "queries": draw_queries(jax.random.fold_in(seeds[12], 71), 0),
        "keys": draw_keys(jax.random.fold_in(seeds[12], 71), 0),
        "values": gaussian(seeds[2], (TOKENS, HEADS * HEAD_DIM), 1.0, 6.0, ((0, 64), (1, 8))),
        "old_keys": gaussian(seeds[3], (OLD, HEADS * HEAD_DIM), 1.0, 6.0, ((0, 64), (1, 8))),
        "old_values": gaussian(seeds[4], (OLD, HEADS * HEAD_DIM), 1.0, 6.0, ((0, 64), (1, 8))),
        "conv_keys": gaussian(seeds[5], (HEADS, 4, HEAD_DIM, HEAD_DIM), (4 * HEAD_DIM) ** -0.5, 0.25, ((0, 8),)),
        "conv_values": gaussian(seeds[6], (HEADS, 4, HEAD_DIM, HEAD_DIM), (4 * HEAD_DIM) ** -0.5, 0.25, ((0, 8),)),
        "out_proj": gaussian(seeds[7], (D, HEADS * HEAD_DIM), (HEADS * HEAD_DIM) ** -0.5, 0.125, ((0, 64), (1, 8))),
        "residual": gaussian(seeds[8], (TOKENS, D), 0.25, 4.0, ((0, 64), (1, 8))),
        "gain": jnp.clip(1.0 + 0.1 * jax.random.normal(seeds[9], (D,), jnp.float32), 0.5, 1.5).astype(jnp.bfloat16),
        "span_order": draw_span_order(jax.random.fold_in(seeds[12], 71), 0),
        "memory_length": jax.random.randint(seeds[11], (1,), CMEM // 4, CMEM + 1).astype(jnp.int32),
    }


def compress(old, conv_weight):
    slots = old.shape[0] // 4
    grouped = old.reshape(slots, 4, HEADS, HEAD_DIM).astype(jnp.float32)
    mixed = jnp.einsum('jthc,htce->jhe', grouped, conv_weight.astype(jnp.float32))
    return mixed.reshape(slots, HEADS * HEAD_DIM).astype(jnp.bfloat16)

def split_heads(array):
    return array.reshape(array.shape[0], HEADS, HEAD_DIM).transpose(1, 0, 2)

def reference(queries, keys, values, old_keys, old_values, conv_keys, conv_values, out_proj, residual, gain, span_order, memory_length):
    half_rows = TOK_DEV // 2
    rows = jnp.arange(TOKENS, dtype=jnp.int32)
    pos = (span_order[rows // half_rows] * half_rows + rows % half_rows).astype(jnp.int32)
    mem_keys = compress(old_keys, conv_keys)
    mem_values = compress(old_values, conv_values)
    mem_ok = jnp.arange(CMEM, dtype=jnp.int32) >= CMEM - memory_length[0]
    scale = 1.0 / math.sqrt(HEAD_DIM)

    def head_out(items):
        query, key_rows, value_rows, mem_k, mem_v = items
        keys_all = jnp.concatenate([mem_k, key_rows], axis=0)
        values_all = jnp.concatenate([mem_v, value_rows], axis=0)
        allowed = jnp.concatenate([jnp.broadcast_to(mem_ok[None, :], (TOKENS, CMEM)), pos[None, :] <= pos[:, None]], axis=1)
        scores = jnp.dot(query, keys_all.T, preferred_element_type=jnp.float32) * scale
        scores = jnp.where(allowed, scores, -1e+30)
        top = lax.optimization_barrier(jnp.max(scores, axis=1))
        weights = jnp.where(allowed, jnp.exp(scores - top[:, None]), 0.0)
        total = lax.optimization_barrier(jnp.sum(weights, axis=1))
        mixed = jnp.dot(weights.astype(jnp.bfloat16), values_all, preferred_element_type=jnp.float32)
        return (mixed / total[:, None]).astype(jnp.bfloat16)
    heads_out = lax.map(head_out, (split_heads(queries), split_heads(keys), split_heads(values), split_heads(mem_keys), split_heads(mem_values)))
    attn = heads_out.transpose(1, 0, 2).reshape(TOKENS, HEADS * HEAD_DIM)
    stream = residual.astype(jnp.float32) + jnp.dot(attn, out_proj.T, preferred_element_type=jnp.float32)
    power = lax.optimization_barrier(jnp.mean(stream * stream, axis=1, keepdims=True))
    normed = stream * lax.rsqrt(power + 1e-06) * gain.astype(jnp.float32)[None, :]
    return normed.astype(jnp.bfloat16)
```

```python
import math

import jax
import jax.numpy as jnp
from jax import lax
from jax.experimental import pallas as pl
from jax.experimental.pallas import tpu as pltpu
from jax.sharding import PartitionSpec as P

MESH = pl.DeviceIdType.MESH
NEG = -1e30
HID = 1e9
F32 = jnp.float32
BF16 = jnp.bfloat16

KV0, WF0, WL0, WS0, QL0, QS0, OO0, OS0, PP0, PW0, COUNT = 0, 8, 16, 19, 21, 24, 28, 35, 42, 49, 56


def dot(a, b, ca, cb):
    return lax.dot_general(a, b, (((ca,), (cb,)), ((), ())), preferred_element_type=F32)


def kernel(
    q_in, k_in, v_in, ok_in, ov_in, ck_in, cv_in, w_in, res_in, gain_in, span_in, mlen_in,
    out_ref,
    kv, qb, wall, kpos, osend, orecv, ssend, srecv, psend, precv, pwsend, pwrecv, attn_s, stream_s,
    ssem, rsem,
):
    ctx = lax.axis_index("ctx")
    dp = lax.axis_index("dp")
    near = lax.rem(ctx, 8)
    far = lax.div(ctx, 8)
    core = lax.rem(near, 2)
    zl = lax.div(near, 2)
    zh = lax.rem(far, 4)
    y = lax.div(far, 4)

    def far_ctx(fy, fz):
        return (fy * 4 + fz) * 8 + near

    def near_ctx(member):
        return far * 8 + member

    zp, zm, zo = lax.rem(zh + 1, 4), lax.rem(zh + 3, 4), lax.rem(zh + 2, 4)
    up, down, other = far_ctx(y, zp), far_ctx(y, zm), far_ctx(1 - y, zh)
    sib = near_ctx(zl * 2 + 1 - core)

    barrier = pltpu.get_barrier_semaphore()
    for peer in (up, down, other):
        pl.semaphore_signal(barrier, inc=1, device_id={"ctx": peer}, device_id_type=MESH)
    for k in range(1, 8):
        pl.semaphore_signal(barrier, inc=1, device_id={"ctx": near_ctx(lax.rem(near + k, 8))}, device_id_type=MESH)
    for k in range(1, 8):
        pl.semaphore_signal(barrier, inc=1, device_id={"dp": lax.rem(dp + k, 8)}, device_id_type=MESH)

    row16 = lax.broadcasted_iota(jnp.int32, (16, 256), 0)
    s0 = span_in[0].astype(F32)
    s1 = span_in[1].astype(F32)
    pick_r = lax.broadcasted_iota(jnp.int32, (16, 32), 0)
    pick_c = lax.broadcasted_iota(jnp.int32, (16, 32), 1)
    for half, (new, old, conv) in enumerate(((k_in, ok_in, ck_in), (v_in, ov_in, cv_in))):
        kv[far, half, 0:128, :] = new[...]
        rows = old[...]
        heads = []
        taps = []
        for t in range(4):
            pick = jnp.where(pick_c == pick_r * 4 + t, 1.0, 0.0).astype(BF16)
            taps.append(dot(pick, rows, 1, 0).astype(BF16))
        for h in range(2):
            total = jnp.zeros((16, 128), F32)
            for t in range(4):
                total = total + dot(taps[t][:, h * 128 : (h + 1) * 128], conv[h, t], 1, 0)
            heads.append(total)
        mem = jnp.concatenate(heads, axis=1)
        if half == 0:
            mem = jnp.where(row16 == 8, s0, jnp.where(row16 == 9, s1, mem))
        kv[far, half, 128:144, :] = mem.astype(BF16)
    qb[near, 0:128, :] = q_in[...]
    qb[near, 128:144, :] = jnp.where(row16 == 0, s0, jnp.where(row16 == 1, s1, 0.0)).astype(BF16)
    wall[far, zl, core] = w_in[...]

    pl.semaphore_wait(barrier, 17)

    def copy(number, ref, dst, where):
        return pltpu.make_async_remote_copy(
            src_ref=ref, dst_ref=dst, send_sem=ssem.at[number], recv_sem=rsem.at[number],
            device_id=where, device_id_type=MESH,
        )

    def same(number, ref, where):
        return copy(number, ref, ref, {"ctx": where})

    def kv_of(fy, fz, part):
        block = kv.at[fy * 4 + fz]
        return block if part is None else block.at[part]

    def w_of(fy, fz, part):
        if part is None:
            return wall.at[fy * 4 + fz, :, core]
        return wall.at[fy * 4 + fz, pl.ds(part * 2, 2), core]

    def send_far(base, of, step):
        for s in step:
            if s == 0:
                same(base, of(y, zh, None), up).start()
            if s == 1:
                same(base + 1, of(y, zh, None), down).start()
            if s == 2:
                same(base + 2, of(y, zh, None), other).start()
            if s == 3:
                same(base + 3, of(y, zm, 0), up).start()
            if s == 4:
                same(base + 4, of(y, zp, 1), down).start()
            if s == 5:
                same(base + 5, of(y, zm, None), other).start()
            if s == 6:
                same(base + 6, of(y, zp, None), other).start()
            if s == 7:
                same(base + 7, of(y, zo, None), other).start()

    def landed(base, of, step):
        blocks = {
            0: (y, zm, None), 1: (y, zp, None), 2: (1 - y, zh, None), 3: (y, zo, 0),
            4: (y, zo, 1), 5: (1 - y, zm, None), 6: (1 - y, zp, None), 7: (1 - y, zo, None),
        }
        for s in step:
            same(base + s, of(*blocks[s]), other).wait_recv()

    send_far(KV0, kv_of, (0, 1, 2))
    for k in (1, 2, 3):
        same(WL0 + k - 1, wall.at[far, zl, core], near_ctx(lax.rem(zl + k, 4) * 2 + core)).start()
    for k in (1, 2, 3):
        same(QL0 + k - 1, qb.at[near], near_ctx(lax.rem(zl + k, 4) * 2 + core)).start()
    same(QS0, qb.at[near], sib).start()

    for k in (1, 2, 3):
        src = lax.rem(zl + 4 - k, 4)
        same(QL0 + k - 1, qb.at[src * 2 + core], sib).wait_recv()
        same(QS0 + k, qb.at[src * 2 + core], sib).start()

    landed(KV0, kv_of, (0,))
    send_far(KV0, kv_of, (3, 5))
    landed(KV0, kv_of, (1,))
    send_far(KV0, kv_of, (4, 6))
    for k in (1, 2, 3):
        same(WL0 + k - 1, wall.at[far, lax.rem(zl + 4 - k, 4), core], sib).wait_recv()
    send_far(WF0, w_of, (0, 1, 2))
    landed(KV0, kv_of, (3, 4))
    send_far(KV0, kv_of, (7,))
    landed(KV0, kv_of, (2, 5, 6, 7))
    same(QS0, qb.at[zl * 2 + 1 - core], sib).wait_recv()
    for k in (1, 2, 3):
        same(QS0 + k, qb.at[lax.rem(zl + 4 - k, 4) * 2 + 1 - core], sib).wait_recv()

    r = lax.broadcasted_iota(jnp.int32, (144, 128), 0)
    rf = r.astype(F32)
    first = (512 - mlen_in[0]).astype(F32)
    for f in range(8):
        tail = kv[f, 0, 128:144, 0:128].astype(F32)
        slot = rf - 128.0 + ((f * 8 + near) * 8).astype(F32)
        mem_pos = jnp.where((slot >= first) & (r < 136), -1.0, HID)
        low = jnp.broadcast_to(tail[8:9] * 64.0, (144, 128)) + rf
        high = jnp.broadcast_to(tail[9:10] * 64.0 - 64.0, (144, 128)) + rf
        kpos[f] = jnp.where(r < 64, low, jnp.where(r < 128, high, mem_pos))

    factor = math.log2(math.e) / math.sqrt(128.0)
    lane = lax.broadcasted_iota(jnp.int32, (8, 128), 1)
    row8 = lax.broadcasted_iota(jnp.int32, (8, 128), 0)

    def attend(m, o_ref, s_ref):
        tail = qb[m, 128:144, 0:128].astype(F32)
        qs0 = jnp.broadcast_to(tail[0:1], (8, 128))
        qs1 = jnp.broadcast_to(tail[1:2], (8, 128))
        qpos = jnp.where(lane < 64, qs0 * 64.0, qs1 * 64.0 - 64.0) + lane.astype(F32)
        vis = kpos[...].reshape(1152, 128) <= qpos[0:1]
        stats = jnp.zeros((8, 128), F32)
        for h in range(2):
            cols = slice(h * 128, (h + 1) * 128)
            keys = kv[:, 0, :, cols].reshape(1152, 128)
            vals = kv[:, 1, :, cols].reshape(1152, 128)
            s = dot(keys, qb[m, 0:128, cols], 1, 1) * factor
            s = jnp.where(vis, s, NEG)
            top = jnp.max(s, axis=0, keepdims=True)
            p = jnp.where(vis, jnp.exp2(s - top), 0.0)
            total = jnp.sum(p, axis=0, keepdims=True)
            o_ref[m if o_ref is osend else near, cols, :] = dot(vals, p.astype(BF16), 0, 0).astype(BF16)
            stats = jnp.where(row8 == h, top, jnp.where(row8 == h + 2, total, stats))
        s_ref[m if s_ref is ssend else near] = stats

    def one(k, carry):
        m = lax.rem(near + k, 8)
        attend(m, osend, ssend)
        copy(OO0 + k - 1, osend.at[m], orecv.at[near], {"ctx": near_ctx(m)}).start()
        copy(OS0 + k - 1, ssend.at[m], srecv.at[near], {"ctx": near_ctx(m)}).start()
        return carry

    lax.fori_loop(1, 5, one, 0)
    landed(WF0, w_of, (0,))
    send_far(WF0, w_of, (3, 5))
    landed(WF0, w_of, (1,))
    send_far(WF0, w_of, (4, 6))
    lax.fori_loop(5, 8, one, 0)
    attend(near, orecv, srecv)

    landed(WF0, w_of, (3, 4))
    send_far(WF0, w_of, (7,))

    def w_half(fy, c):
        return wall.at[pl.ds(fy * 4, 4), :, c]

    same(WS0, w_half(y, core), sib).start()
    landed(WF0, w_of, (2, 5, 6, 7))
    same(WS0 + 1, w_half(1 - y, core), sib).start()

    for k in range(1, 8):
        src = lax.rem(near + 8 - k, 8)
        copy(OO0 + k - 1, osend.at[src], orecv.at[src], {"ctx": sib}).wait_recv()
        copy(OS0 + k - 1, ssend.at[src], srecv.at[src], {"ctx": sib}).wait_recv()

    for h in range(2):
        cols = slice(h * 128, (h + 1) * 128)
        tops = srecv[:, h, :]
        sums = srecv[:, h + 2, :]
        best = jnp.max(tops, axis=0, keepdims=True)
        weight = jnp.exp2(tops - best)
        total = jnp.sum(weight * sums, axis=0, keepdims=True)
        acc = jnp.zeros((128, 128), F32)
        for j in range(8):
            acc = acc + orecv[j, cols, :].astype(F32) * weight[j : j + 1]
        attn_s[:, cols] = (acc / total).T.astype(BF16)

    same(WS0, w_half(y, 1 - core), sib).wait_recv()
    same(WS0 + 1, w_half(1 - y, 1 - core), sib).wait_recv()

    def project(g):
        return dot(attn_s[...], wall[g].reshape(512, 256), 1, 1)

    def push(k, carry):
        g = lax.rem(dp + k, 8)
        psend[g] = project(g).astype(BF16)
        copy(PP0 + k - 1, psend.at[g], precv.at[dp], {"dp": g}).start()
        return carry

    lax.fori_loop(1, 8, push, 0)
    stream_s[...] = res_in[...].astype(F32) + project(dp)
    for k in range(1, 8):
        src = lax.rem(dp + 8 - k, 8)
        copy(PP0 + k - 1, psend.at[src], precv.at[src], {"dp": src}).wait_recv()
        stream_s[...] += precv[src].astype(F32)

    stream = stream_s[...]
    mine = jnp.sum(stream * stream, axis=1, keepdims=True)
    line = jnp.broadcast_to(mine, (128, 128)).T
    pwsend[...] = line[0:8]
    pwrecv[dp] = line[0:8]
    for k in range(1, 8):
        copy(PW0 + k - 1, pwsend, pwrecv.at[dp], {"dp": lax.rem(dp + k, 8)}).start()
    for k in range(1, 8):
        src = lax.rem(dp + 8 - k, 8)
        copy(PW0 + k - 1, pwsend, pwrecv.at[src], {"dp": src}).wait_recv()
    power = jnp.sum(pwrecv[...], axis=0)[0:1] / 4096.0
    norm = jnp.broadcast_to(lax.rsqrt(power + 1e-6), (128, 128)).T
    gain = gain_in[...].astype(F32)
    for c in range(4):
        cols = slice(c * 128, (c + 1) * 128)
        out_ref[:, cols] = (stream_s[:, cols] * norm * gain[:, cols]).astype(BF16)

    for s in range(8):
        whole = s not in (3, 4)
        same(KV0 + s, kv_of(y, zh, None if whole else 0), other).wait_send()
        same(WF0 + s, w_of(y, zh, None if whole else 0), other).wait_send()
    for k in range(3):
        same(WL0 + k, wall.at[far, zl, core], sib).wait_send()
        same(QL0 + k, qb.at[near], sib).wait_send()
    for k in range(4):
        same(QS0 + k, qb.at[near], sib).wait_send()
    same(WS0, w_half(y, core), sib).wait_send()
    same(WS0 + 1, w_half(1 - y, core), sib).wait_send()
    for k in range(7):
        copy(OO0 + k, osend.at[0], orecv.at[near], {"ctx": sib}).wait_send()
        copy(OS0 + k, ssend.at[0], srecv.at[near], {"ctx": sib}).wait_send()
        copy(PP0 + k, psend.at[0], precv.at[dp], {"ctx": sib}).wait_send()
        copy(PW0 + k, pwsend, pwrecv.at[dp], {"ctx": sib}).wait_send()


def local(
    queries, keys, values, old_keys, old_values, conv_keys, conv_values, out_proj, residual, gain,
    span_order, memory_length,
):
    vm = pl.BlockSpec(memory_space=pltpu.VMEM)
    sm = pl.BlockSpec(memory_space=pltpu.SMEM)
    return pl.pallas_call(
        kernel,
        out_shape=jax.ShapeDtypeStruct(residual.shape, BF16),
        in_specs=[vm] * 10 + [sm] * 2,
        out_specs=vm,
        scratch_shapes=[
            pltpu.VMEM((8, 2, 144, 256), BF16),
            pltpu.VMEM((8, 144, 256), BF16),
            pltpu.VMEM((8, 4, 2, 64, 256), BF16),
            pltpu.VMEM((8, 144, 128), F32),
            pltpu.VMEM((8, 256, 128), BF16),
            pltpu.VMEM((8, 256, 128), BF16),
            pltpu.VMEM((8, 8, 128), F32),
            pltpu.VMEM((8, 8, 128), F32),
            pltpu.VMEM((8, 128, 512), BF16),
            pltpu.VMEM((8, 128, 512), BF16),
            pltpu.VMEM((8, 128), F32),
            pltpu.VMEM((8, 8, 128), F32),
            pltpu.VMEM((128, 256), BF16),
            pltpu.VMEM((128, 512), F32),
            pltpu.SemaphoreType.DMA((COUNT,)),
            pltpu.SemaphoreType.DMA((COUNT,)),
        ],
        compiler_params=pltpu.CompilerParams(collective_id=0, has_side_effects=True),
    )(
        queries, keys, values, old_keys, old_values, conv_keys, conv_values, out_proj, residual,
        gain.reshape(1, -1), span_order, memory_length,
    )


def solution(mesh):
    placed = (
        P("ctx", "dp"),
        P("ctx", "dp"),
        P("ctx", "dp"),
        P("ctx", "dp"),
        P("ctx", "dp"),
        P("dp", None, None, None),
        P("dp", None, None, None),
        P("ctx", "dp"),
        P("ctx", "dp"),
        P("dp"),
        P("ctx"),
        P(),
    )
    return jax.shard_map(
        local, mesh=mesh, in_specs=placed, out_specs=P("ctx", "dp"), check_vma=False
    )
```

```python
import math

import jax
import jax.numpy as jnp
from jax import lax
from jax.experimental import pallas as pl
from jax.experimental.pallas import tpu as pltpu
from jax.sharding import PartitionSpec as P

MESH = pl.DeviceIdType.MESH
NEG = -1e30
HID = 1e9
F32 = jnp.float32
BF16 = jnp.bfloat16

KU, KD, VU, VD, WU, WD = 0, 8, 16, 24, 32, 40
SU, SD, SX, QQ, WY, OO, OS, PP, PW, COUNT = 48, 56, 64, 66, 69, 70, 73, 76, 83, 90


def dot(a, b, ca, cb):
    return lax.dot_general(a, b, (((ca,), (cb,)), ((), ())), preferred_element_type=F32)


def kernel(
    q_in, k_in, v_in, ok_in, ov_in, ck_in, cv_in, w_in, res_in, gain_in, span_in, mlen_in,
    out_ref,
    kv, qb, wall, acc, rows, osend, orecv, ssend, srecv, psend, precv, pwsend, pwrecv, attn_s, stream_s,
    ssem, rsem,
):
    ctx = lax.axis_index("ctx")
    dp = lax.axis_index("dp")
    core = lax.rem(ctx, 2)
    z = lax.rem(lax.div(ctx, 2), 16)
    y = lax.div(ctx, 32)
    me = y * 2 + core

    def at(fy, fz, fc):
        return (fy * 16 + fz) * 2 + fc

    def behind(s):
        return lax.rem(z + 16 - s, 16)

    def ahead(s):
        return lax.rem(z + s, 16)

    up, down = at(y, ahead(1), core), at(y, behind(1), core)
    sib, other, cross = at(y, z, 1 - core), at(1 - y, z, core), at(1 - y, z, 1 - core)

    barrier = pltpu.get_barrier_semaphore()
    for peer in (up, down, sib, other, cross):
        pl.semaphore_signal(barrier, inc=1, device_id={"ctx": peer}, device_id_type=MESH)
    for k in range(1, 8):
        pl.semaphore_signal(barrier, inc=1, device_id={"dp": lax.rem(dp + k, 8)}, device_id_type=MESH)

    row16 = lax.broadcasted_iota(jnp.int32, (16, 256), 0)
    s0 = span_in[0].astype(F32)
    s1 = span_in[1].astype(F32)
    pick_r = lax.broadcasted_iota(jnp.int32, (16, 32), 0)
    pick_c = lax.broadcasted_iota(jnp.int32, (16, 32), 1)
    for half, (new, old, conv) in enumerate(((k_in, ok_in, ck_in), (v_in, ov_in, cv_in))):
        kv[z, half, 0:128, :] = new[...]
        taps = []
        for t in range(4):
            pick = jnp.where(pick_c == pick_r * 4 + t, 1.0, 0.0).astype(BF16)
            taps.append(dot(pick, old[...], 1, 0).astype(BF16))
        heads = []
        for h in range(2):
            total = jnp.zeros((16, 128), F32)
            for t in range(4):
                total = total + dot(taps[t][:, h * 128 : (h + 1) * 128], conv[h, t], 1, 0)
            heads.append(total)
        mem = jnp.concatenate(heads, axis=1)
        if half == 0:
            mem = jnp.where(row16 == 8, s0, jnp.where(row16 == 9, s1, mem))
        kv[z, half, 128:144, :] = mem.astype(BF16)
    qb[me, 0:128, :] = q_in[...]
    qb[me, 128:144, :] = jnp.where(row16 == 0, s0, jnp.where(row16 == 1, s1, 0.0)).astype(BF16)
    wall[y, z, core] = w_in[...]
    acc[...] = jnp.zeros_like(acc)
    rows[...] = jnp.where(lax.broadcasted_iota(jnp.int32, (8, 512), 0) < 2, NEG, 0.0)

    pl.semaphore_wait(barrier, 12)

    def copy(number, ref, dst, where):
        return pltpu.make_async_remote_copy(
            src_ref=ref, dst_ref=dst, send_sem=ssem.at[number], recv_sem=rsem.at[number],
            device_id=where, device_id_type=MESH,
        )

    def same(number, ref, where):
        return copy(number, ref, ref, {"ctx": where})

    def w_of(fz, c):
        return wall.at[:, fz, c]

    same(WY, wall.at[y, z, core], other).start()
    same(KU, kv.at[z, 0], up).start()
    same(KD, kv.at[z, 0], down).start()
    for k, peer in enumerate((other, cross, sib)):
        same(QQ + k, qb.at[me], peer).start()
    same(VU, kv.at[z, 1], up).start()
    same(VD, kv.at[z, 1], down).start()
    same(WY, wall.at[1 - y, z, core], other).wait_recv()
    same(WU, w_of(z, core), up).start()
    same(WD, w_of(z, core), down).start()
    same(SX, w_of(z, core), sib).start()
    for k, (fy, fc) in enumerate(((1 - y, core), (1 - y, 1 - core), (y, 1 - core))):
        same(QQ + k, qb.at[fy * 2 + fc], other).wait_recv()

    factor = math.log2(math.e) / math.sqrt(128.0)
    r = lax.broadcasted_iota(jnp.int32, (144, 128), 0)
    rf = r.astype(F32)
    first = (512 - mlen_in[0]).astype(F32)
    lane = lax.broadcasted_iota(jnp.int32, (8, 128), 1)

    def positions(fz):
        tail = kv[fz, 0, 128:144, 0:128].astype(F32)
        slot = rf - 128.0 + (at(y, fz, core) * 8).astype(F32)
        mem_pos = jnp.where((slot >= first) & (r < 136), -1.0, HID)
        low = jnp.broadcast_to(tail[8:9] * 64.0, (144, 128)) + rf
        high = jnp.broadcast_to(tail[9:10] * 64.0 - 64.0, (144, 128)) + rf
        place = jnp.where(r < 64, low, jnp.where(r < 128, high, mem_pos))
        return jnp.concatenate([place] * 4, axis=1)

    def fold(blocks):
        parts = []
        for m in range(4):
            tail = qb[m, 128:144, 0:128].astype(F32)
            q0 = jnp.broadcast_to(tail[0:1], (8, 128))
            q1 = jnp.broadcast_to(tail[1:2], (8, 128))
            parts.append(jnp.where(lane < 64, q0 * 64.0, q1 * 64.0 - 64.0) + lane.astype(F32))
        qpos = jnp.concatenate(parts, axis=1)[0:1]
        vis = jnp.concatenate([positions(b) for b in blocks], axis=0) <= qpos
        for h in range(2):
            cols = slice(h * 128, (h + 1) * 128)
            keys = jnp.concatenate([kv[b, 0, :, cols] for b in blocks], axis=0)
            vals = jnp.concatenate([kv[b, 1, :, cols] for b in blocks], axis=0)
            s = dot(keys, qb[:, 0:128, cols].reshape(512, 128), 1, 1) * factor
            s = jnp.where(vis, s, NEG)
            before = rows[h : h + 1, :]
            top = jnp.maximum(before, jnp.max(s, axis=0, keepdims=True))
            p = jnp.where(vis, jnp.exp2(s - top), 0.0)
            shrink = jnp.exp2(before - top)
            rows[h : h + 1, :] = top
            rows[h + 2 : h + 3, :] = rows[h + 2 : h + 3, :] * shrink + jnp.sum(p, axis=0, keepdims=True)
            acc[cols, :] = acc[cols, :] * shrink + dot(vals, p.astype(BF16), 0, 0)

    fold([z])

    def stage(s, carry):
        lo, hi = behind(s), ahead(s)
        for base, half, at_z, to in ((KU, 0, lo, up), (KD, 0, hi, down), (VU, 1, lo, up), (VD, 1, hi, down)):
            same(base + s - 1, kv.at[at_z, half], to).wait_recv()
            same(base + s, kv.at[at_z, half], to).start()
        fold([lo, hi])
        for base, side, at_z, to in ((WU, SU, lo, up), (WD, SD, hi, down)):
            same(base + s - 1, w_of(at_z, core), to).wait_recv()
            same(base + s, w_of(at_z, core), to).start()
            same(side + s - 1, w_of(at_z, core), sib).start()
        return carry

    lax.fori_loop(1, 7, stage, 0)
    lo, hi, far = behind(7), ahead(7), ahead(8)
    for base, half, at_z, to in ((KU, 0, lo, up), (KD, 0, hi, down), (VU, 1, lo, up), (VD, 1, hi, down)):
        same(base + 6, kv.at[at_z, half], to).wait_recv()
        if base in (KU, VD):
            same(base + 7, kv.at[at_z, half], to).start()
    fold([lo, hi])
    for base, side, at_z, to, fy in ((WU, SU, lo, up, 0), (WD, SD, hi, down, 1)):
        same(base + 6, w_of(at_z, core), to).wait_recv()
        same(base + 7, wall.at[fy, at_z, core], to).start()
        same(side + 6, w_of(at_z, core), sib).start()
    same(KU + 7, kv.at[far, 0], up).wait_recv()
    same(VD + 7, kv.at[far, 1], down).wait_recv()
    fold([far])

    for k, (fy, fc) in enumerate(((1 - y, core), (1 - y, 1 - core), (y, 1 - core))):
        m = fy * 2 + fc
        peer = (other, cross, sib)[k]
        lanes = pl.ds(pl.multiple_of(m * 128, 128), 128)
        osend[k] = acc[:, lanes].astype(BF16)
        ssend[k] = rows[:, lanes]
        copy(OO + k, osend.at[k], orecv.at[k], {"ctx": peer}).start()
        copy(OS + k, ssend.at[k], srecv.at[k], {"ctx": peer}).start()
    lanes = pl.ds(pl.multiple_of(me * 128, 128), 128)
    srecv[3] = rows[:, lanes]

    for base, fy in ((WU, 0), (WD, 1)):
        same(base + 7, wall.at[fy, far, core], up).wait_recv()
    same(SX + 1, w_of(far, core), sib).start()

    for k in range(3):
        copy(OO + k, osend.at[k], orecv.at[k], {"ctx": sib}).wait_recv()
        copy(OS + k, ssend.at[k], srecv.at[k], {"ctx": sib}).wait_recv()
    for h in range(2):
        cols = slice(h * 128, (h + 1) * 128)
        tops = srecv[:, h, :]
        sums = srecv[:, h + 2, :]
        best = jnp.max(tops, axis=0, keepdims=True)
        weight = jnp.exp2(tops - best)
        total = jnp.sum(weight * sums, axis=0, keepdims=True)
        mixed = acc[cols, lanes] * weight[3:4]
        for j in range(3):
            mixed = mixed + orecv[j, cols, :].astype(F32) * weight[j : j + 1]
        attn_s[:, cols] = (mixed / total).T.astype(BF16)

    for s in range(1, 8):
        same(SU + s - 1, w_of(behind(s), 1 - core), sib).wait_recv()
        same(SD + s - 1, w_of(ahead(s), 1 - core), sib).wait_recv()
    same(SX, w_of(z, 1 - core), sib).wait_recv()
    same(SX + 1, w_of(far, 1 - core), sib).wait_recv()

    def project(g):
        block = wall[lax.div(g, 4), pl.ds(lax.rem(g, 4) * 4, 4)]
        return dot(attn_s[...], block.reshape(512, 256), 1, 1)

    def push(k, carry):
        g = lax.rem(dp + k, 8)
        psend[g] = project(g).astype(BF16)
        copy(PP + k - 1, psend.at[g], precv.at[dp], {"dp": g}).start()
        return carry

    lax.fori_loop(1, 8, push, 0)
    stream_s[...] = res_in[...].astype(F32) + project(dp)
    for k in range(1, 8):
        src = lax.rem(dp + 8 - k, 8)
        copy(PP + k - 1, psend.at[src], precv.at[src], {"dp": src}).wait_recv()
        stream_s[...] += precv[src].astype(F32)

    stream = stream_s[...]
    mine = jnp.sum(stream * stream, axis=1, keepdims=True)
    line = jnp.broadcast_to(mine, (128, 128)).T
    pwsend[...] = line[0:8]
    pwrecv[dp] = line[0:8]
    for k in range(1, 8):
        copy(PW + k - 1, pwsend, pwrecv.at[dp], {"dp": lax.rem(dp + k, 8)}).start()
    for k in range(1, 8):
        src = lax.rem(dp + 8 - k, 8)
        copy(PW + k - 1, pwsend, pwrecv.at[src], {"dp": src}).wait_recv()
    power = jnp.sum(pwrecv[...], axis=0)[0:1] / 4096.0
    norm = jnp.broadcast_to(lax.rsqrt(power + 1e-6), (128, 128)).T
    gain = gain_in[...].astype(F32)
    for c in range(4):
        cols = slice(c * 128, (c + 1) * 128)
        out_ref[:, cols] = (stream_s[:, cols] * norm * gain[:, cols]).astype(BF16)

    for s in range(8):
        if s < 7:
            same(VU + s, kv.at[z, 1], up).wait_send()
            same(KD + s, kv.at[z, 0], up).wait_send()
            same(SU + s, w_of(z, core), sib).wait_send()
            same(SD + s, w_of(z, core), sib).wait_send()
        same(KU + s, kv.at[z, 0], up).wait_send()
        same(VD + s, kv.at[z, 1], up).wait_send()
        for base in (WU, WD):
            same(base + s, w_of(z, core) if s < 7 else wall.at[0, z, core], up).wait_send()
    same(SX, w_of(z, core), sib).wait_send()
    same(SX + 1, w_of(z, core), sib).wait_send()
    same(WY, wall.at[y, z, core], other).wait_send()
    for k in range(3):
        same(QQ + k, qb.at[me], sib).wait_send()
        copy(OO + k, osend.at[k], orecv.at[k], {"ctx": sib}).wait_send()
        copy(OS + k, ssend.at[k], srecv.at[k], {"ctx": sib}).wait_send()
    for k in range(7):
        copy(PP + k, psend.at[0], precv.at[dp], {"ctx": sib}).wait_send()
        copy(PW + k, pwsend, pwrecv.at[dp], {"ctx": sib}).wait_send()


def local(
    queries, keys, values, old_keys, old_values, conv_keys, conv_values, out_proj, residual, gain,
    span_order, memory_length,
):
    vm = pl.BlockSpec(memory_space=pltpu.VMEM)
    sm = pl.BlockSpec(memory_space=pltpu.SMEM)
    return pl.pallas_call(
        kernel,
        out_shape=jax.ShapeDtypeStruct(residual.shape, BF16),
        in_specs=[vm] * 10 + [sm] * 2,
        out_specs=vm,
        scratch_shapes=[
            pltpu.VMEM((16, 2, 144, 256), BF16),
            pltpu.VMEM((4, 144, 256), BF16),
            pltpu.VMEM((2, 16, 2, 64, 256), BF16),
            pltpu.VMEM((256, 512), F32),
            pltpu.VMEM((8, 512), F32),
            pltpu.VMEM((3, 256, 128), BF16),
            pltpu.VMEM((3, 256, 128), BF16),
            pltpu.VMEM((3, 8, 128), F32),
            pltpu.VMEM((4, 8, 128), F32),
            pltpu.VMEM((8, 128, 512), BF16),
            pltpu.VMEM((8, 128, 512), BF16),
            pltpu.VMEM((8, 128), F32),
            pltpu.VMEM((8, 8, 128), F32),
            pltpu.VMEM((128, 256), BF16),
            pltpu.VMEM((128, 512), F32),
            pltpu.SemaphoreType.DMA((COUNT,)),
            pltpu.SemaphoreType.DMA((COUNT,)),
        ],
        compiler_params=pltpu.CompilerParams(collective_id=0, has_side_effects=True),
    )(
        queries, keys, values, old_keys, old_values, conv_keys, conv_values, out_proj, residual,
        gain.reshape(1, -1), span_order, memory_length,
    )


def solution(mesh):
    placed = (
        P("ctx", "dp"),
        P("ctx", "dp"),
        P("ctx", "dp"),
        P("ctx", "dp"),
        P("ctx", "dp"),
        P("dp", None, None, None),
        P("dp", None, None, None),
        P("ctx", "dp"),
        P("ctx", "dp"),
        P("dp"),
        P("ctx"),
        P(),
    )
    return jax.shard_map(
        local, mesh=mesh, in_specs=placed, out_specs=P("ctx", "dp"), check_vma=False
    )
```

```python
import math

import jax
import jax.numpy as jnp
from jax import lax
from jax.experimental import pallas as pl
from jax.experimental.pallas import tpu as pltpu
from jax.sharding import PartitionSpec as P

MESH = pl.DeviceIdType.MESH
NEG = -1e30
HID = 1e9
F32 = jnp.float32
BF16 = jnp.bfloat16

KU, KD, WU, WD, SU, SD, SX, QQ, WY = 0, 32, 64, 72, 80, 88, 96, 98, 101
OO, OS, PW, RL, RF, PD, COUNT = 102, 105, 108, 115, 119, 123, 128


def dot(a, b, ca, cb):
    return lax.dot_general(a, b, (((ca,), (cb,)), ((), ())), preferred_element_type=F32)


def kernel(
    q_in, k_in, v_in, ok_in, ov_in, ck_in, cv_in, w_in, res_in, gain_in, span_in, mlen_in,
    out_ref,
    kv, qb, wall, acc, rows, osend, orecv, ssend, srecv, psend, precv, relay, pwsend, pwrecv, attn_s, stream_s,
    ssem, rsem,
):
    ctx = lax.axis_index("ctx")
    dp = lax.axis_index("dp")
    core = lax.rem(ctx, 2)
    z = lax.rem(lax.div(ctx, 2), 16)
    y = lax.div(ctx, 32)
    me = y * 2 + core

    def at(fy, fz, fc):
        return (fy * 16 + fz) * 2 + fc

    def behind(s):
        return lax.rem(z + 16 - s, 16)

    def ahead(s):
        return lax.rem(z + s, 16)

    up, down = at(y, ahead(1), core), at(y, behind(1), core)
    sib, other, cross = at(y, z, 1 - core), at(1 - y, z, core), at(1 - y, z, 1 - core)

    barrier = pltpu.get_barrier_semaphore()
    for peer in (up, down, sib, other, cross):
        pl.semaphore_signal(barrier, inc=1, device_id={"ctx": peer}, device_id_type=MESH)
    for k in range(1, 8):
        pl.semaphore_signal(barrier, inc=1, device_id={"dp": lax.rem(dp + k, 8)}, device_id_type=MESH)

    row16 = lax.broadcasted_iota(jnp.int32, (16, 256), 0)
    s0 = span_in[0].astype(F32)
    s1 = span_in[1].astype(F32)
    pick_r = lax.broadcasted_iota(jnp.int32, (16, 32), 0)
    pick_c = lax.broadcasted_iota(jnp.int32, (16, 32), 1)
    for half, (new, old, conv) in enumerate(((k_in, ok_in, ck_in), (v_in, ov_in, cv_in))):
        for h in range(2):
            kv[z, half * 2 + h, 0:128, :] = new[:, h * 128 : (h + 1) * 128]
        taps = []
        for t in range(4):
            pick = jnp.where(pick_c == pick_r * 4 + t, 1.0, 0.0).astype(BF16)
            taps.append(dot(pick, old[...], 1, 0).astype(BF16))
        heads = []
        for h in range(2):
            total = jnp.zeros((16, 128), F32)
            for t in range(4):
                total = total + dot(taps[t][:, h * 128 : (h + 1) * 128], conv[h, t], 1, 0)
            heads.append(total)
        mem = jnp.concatenate(heads, axis=1)
        if half == 0:
            mem = jnp.where(row16 == 8, s0, jnp.where(row16 == 9, s1, mem))
        for h in range(2):
            kv[z, half * 2 + h, 128:144, :] = mem[:, h * 128 : (h + 1) * 128].astype(BF16)
    qb[me, 0:128, :] = q_in[...]
    qb[me, 128:144, :] = jnp.where(row16 == 0, s0, jnp.where(row16 == 1, s1, 0.0)).astype(BF16)
    wall[y, z, core] = w_in[...]
    acc[...] = jnp.zeros_like(acc)
    rows[...] = jnp.where(lax.broadcasted_iota(jnp.int32, (8, 512), 0) < 2, NEG, 0.0)

    pl.semaphore_wait(barrier, 12)

    def copy(number, ref, dst, where):
        return pltpu.make_async_remote_copy(
            src_ref=ref, dst_ref=dst, send_sem=ssem.at[number], recv_sem=rsem.at[number],
            device_id=where, device_id_type=MESH,
        )

    def same(number, ref, where):
        return copy(number, ref, ref, {"ctx": where})

    def w_of(fz, c):
        return wall.at[:, fz, c]

    same(WY, wall.at[y, z, core], other).start()
    for c in (0, 1):
        same(KU + c * 8, kv.at[z, c], up).start()
        same(KD + c * 8, kv.at[z, c], down).start()
    for k, peer in enumerate((other, cross, sib)):
        same(QQ + k, qb.at[me], peer).start()
    for c in (2, 3):
        same(KU + c * 8, kv.at[z, c], up).start()
        same(KD + c * 8, kv.at[z, c], down).start()
    same(WY, wall.at[1 - y, z, core], other).wait_recv()
    same(WU, w_of(z, core), up).start()
    same(WD, w_of(z, core), down).start()
    same(SX, w_of(z, core), sib).start()
    for k, (fy, fc) in enumerate(((1 - y, core), (1 - y, 1 - core), (y, 1 - core))):
        same(QQ + k, qb.at[fy * 2 + fc], other).wait_recv()

    factor = math.log2(math.e) / math.sqrt(128.0)
    r = lax.broadcasted_iota(jnp.int32, (144, 128), 0)
    rf = r.astype(F32)
    first = (512 - mlen_in[0]).astype(F32)
    lane = lax.broadcasted_iota(jnp.int32, (8, 128), 1)

    def positions(fz):
        tail = kv[fz, 0, 128:144, :].astype(F32)
        slot = rf - 128.0 + (at(y, fz, core) * 8).astype(F32)
        mem_pos = jnp.where((slot >= first) & (r < 136), -1.0, HID)
        low = jnp.broadcast_to(tail[8:9] * 64.0, (144, 128)) + rf
        high = jnp.broadcast_to(tail[9:10] * 64.0 - 64.0, (144, 128)) + rf
        place = jnp.where(r < 64, low, jnp.where(r < 128, high, mem_pos))
        return jnp.concatenate([place] * 4, axis=1)

    def fold(blocks):
        parts = []
        for m in range(4):
            tail = qb[m, 128:144, 0:128].astype(F32)
            q0 = jnp.broadcast_to(tail[0:1], (8, 128))
            q1 = jnp.broadcast_to(tail[1:2], (8, 128))
            parts.append(jnp.where(lane < 64, q0 * 64.0, q1 * 64.0 - 64.0) + lane.astype(F32))
        qpos = jnp.concatenate(parts, axis=1)[0:1]
        vis = jnp.concatenate([positions(b) for b in blocks], axis=0) <= qpos
        for h in range(2):
            cols = slice(h * 128, (h + 1) * 128)
            keys = jnp.concatenate([kv[b, h] for b in blocks], axis=0)
            vals = jnp.concatenate([kv[b, 2 + h] for b in blocks], axis=0)
            s = dot(keys, qb[:, 0:128, cols].reshape(512, 128), 1, 1) * factor
            s = jnp.where(vis, s, NEG)
            before = rows[h : h + 1, :]
            top = jnp.maximum(before, jnp.max(s, axis=0, keepdims=True))
            p = jnp.where(vis, jnp.exp2(s - top), 0.0)
            shrink = jnp.exp2(before - top)
            rows[h : h + 1, :] = top
            rows[h + 2 : h + 3, :] = rows[h + 2 : h + 3, :] * shrink + jnp.sum(p, axis=0, keepdims=True)
            acc[cols, :] = acc[cols, :] * shrink + dot(vals, p.astype(BF16), 0, 0)

    fold([z])

    def stage(s, carry):
        lo, hi = behind(s), ahead(s)
        for c in range(4):
            for base, at_z, to in ((KU + c * 8, lo, up), (KD + c * 8, hi, down)):
                same(base + s - 1, kv.at[at_z, c], to).wait_recv()
                same(base + s, kv.at[at_z, c], to).start()
        fold([lo, hi])
        for base, side, at_z, to in ((WU, SU, lo, up), (WD, SD, hi, down)):
            same(base + s - 1, w_of(at_z, core), to).wait_recv()
            same(base + s, w_of(at_z, core), to).start()
            same(side + s - 1, w_of(at_z, core), sib).start()
        return carry

    lax.fori_loop(1, 7, stage, 0)
    lo, hi, far = behind(7), ahead(7), ahead(8)
    for c in range(4):
        for base, at_z, to in ((KU + c * 8, lo, up), (KD + c * 8, hi, down)):
            same(base + 6, kv.at[at_z, c], to).wait_recv()
            if (to is up) == (c % 2 == 0):
                same(base + 7, kv.at[at_z, c], to).start()
    fold([lo, hi])
    for base, side, at_z, to, fy in ((WU, SU, lo, up, 0), (WD, SD, hi, down, 1)):
        same(base + 6, w_of(at_z, core), to).wait_recv()
        same(base + 7, wall.at[fy, at_z, core], to).start()
        same(side + 6, w_of(at_z, core), sib).start()
    for c in range(4):
        same((KD if c % 2 else KU) + c * 8 + 7, kv.at[far, c], up).wait_recv()
    fold([far])

    for k, (fy, fc) in enumerate(((1 - y, core), (1 - y, 1 - core), (y, 1 - core))):
        m = fy * 2 + fc
        peer = (other, cross, sib)[k]
        lanes = pl.ds(pl.multiple_of(m * 128, 128), 128)
        osend[k] = acc[:, lanes].astype(BF16)
        ssend[k] = rows[:, lanes]
        copy(OO + k, osend.at[k], orecv.at[k], {"ctx": peer}).start()
        copy(OS + k, ssend.at[k], srecv.at[k], {"ctx": peer}).start()
    lanes = pl.ds(pl.multiple_of(me * 128, 128), 128)
    srecv[3] = rows[:, lanes]

    for base, fy in ((WU, 0), (WD, 1)):
        same(base + 7, wall.at[fy, far, core], up).wait_recv()
    same(SX + 1, w_of(far, core), sib).start()

    for k in range(3):
        copy(OO + k, osend.at[k], orecv.at[k], {"ctx": sib}).wait_recv()
        copy(OS + k, ssend.at[k], srecv.at[k], {"ctx": sib}).wait_recv()
    for h in range(2):
        cols = slice(h * 128, (h + 1) * 128)
        tops = srecv[:, h, :]
        sums = srecv[:, h + 2, :]
        best = jnp.max(tops, axis=0, keepdims=True)
        weight = jnp.exp2(tops - best)
        total = jnp.sum(weight * sums, axis=0, keepdims=True)
        mixed = acc[cols, lanes] * weight[3:4]
        for j in range(3):
            mixed = mixed + orecv[j, cols, :].astype(F32) * weight[j : j + 1]
        attn_s[:, cols] = (mixed / total).T.astype(BF16)

    for s in range(1, 8):
        same(SU + s - 1, w_of(behind(s), 1 - core), sib).wait_recv()
        same(SD + s - 1, w_of(ahead(s), 1 - core), sib).wait_recv()
    same(SX, w_of(z, 1 - core), sib).wait_recv()
    same(SX + 1, w_of(far, 1 - core), sib).wait_recv()

    def project(g):
        block = wall[lax.div(g, 4), pl.ds(lax.rem(g, 4) * 4, 4)]
        return dot(attn_s[...], block.reshape(512, 256), 1, 1)

    px = lax.div(dp, 2)
    py = lax.rem(dp, 2)

    def dp_at(dx, flip):
        return lax.rem(px + 4 + dx, 4) * 2 + (1 - py if flip else py)

    for flip in (0, 1):
        g = dp_at(2, flip)
        psend[g] = project(g).astype(BF16)
        for way, dx in ((0, 1), (1, -1)):
            copy(RL + way * 2 + flip, psend.at[g, pl.ds(way * 64, 64)], relay.at[way * 2 + flip], {"dp": dp_at(dx, flip)}).start()
    straight = ((1, 0), (-1, 0), (1, 1), (-1, 1), (0, 1))
    for n, (dx, flip) in enumerate(straight):
        g = dp_at(dx, flip)
        psend[g] = project(g).astype(BF16)
        copy(PD + n, psend.at[g], precv.at[dp], {"dp": g}).start()
    for flip in (0, 1):
        for way, dx in ((0, 1), (1, -1)):
            n = way * 2 + flip
            copy(RL + n, relay.at[n], relay.at[n], {"dp": dp_at(dx, 0)}).wait_recv()
            copy(RF + n, relay.at[n], precv.at[dp_at(-dx, flip), pl.ds(way * 64, 64)], {"dp": dp_at(dx, 0)}).start()
    stream_s[...] = res_in[...].astype(F32) + project(dp)
    for n, (dx, flip) in enumerate(straight):
        src = dp_at(-dx, flip)
        copy(PD + n, psend.at[src], precv.at[src], {"dp": dp_at(1, 0)}).wait_recv()
        stream_s[...] += precv[src].astype(F32)
    for flip in (0, 1):
        src = dp_at(2, flip)
        for way in (0, 1):
            n = way * 2 + flip
            copy(RF + n, relay.at[n], precv.at[src, pl.ds(way * 64, 64)], {"dp": dp_at(1, 0)}).wait_recv()
        stream_s[...] += precv[src].astype(F32)

    stream = stream_s[...]
    mine = jnp.sum(stream * stream, axis=1, keepdims=True)
    line = jnp.broadcast_to(mine, (128, 128)).T
    pwsend[...] = line[0:8]
    pwrecv[dp] = line[0:8]
    for k in range(1, 8):
        copy(PW + k - 1, pwsend, pwrecv.at[dp], {"dp": lax.rem(dp + k, 8)}).start()
    for k in range(1, 8):
        src = lax.rem(dp + 8 - k, 8)
        copy(PW + k - 1, pwsend, pwrecv.at[src], {"dp": src}).wait_recv()
    power = jnp.sum(pwrecv[...], axis=0)[0:1] / 4096.0
    norm = jnp.broadcast_to(lax.rsqrt(power + 1e-6), (128, 128)).T
    gain = gain_in[...].astype(F32)
    for c in range(4):
        cols = slice(c * 128, (c + 1) * 128)
        out_ref[:, cols] = (stream_s[:, cols] * norm * gain[:, cols]).astype(BF16)

    for s in range(8):
        for c in range(4):
            for base in (KU, KD):
                if s < 7 or (base == KU) == (c % 2 == 0):
                    same(base + c * 8 + s, kv.at[z, c], up).wait_send()
        if s < 7:
            same(SU + s, w_of(z, core), sib).wait_send()
            same(SD + s, w_of(z, core), sib).wait_send()
        for base in (WU, WD):
            same(base + s, w_of(z, core) if s < 7 else wall.at[0, z, core], up).wait_send()
    same(SX, w_of(z, core), sib).wait_send()
    same(SX + 1, w_of(z, core), sib).wait_send()
    same(WY, wall.at[y, z, core], other).wait_send()
    for k in range(3):
        same(QQ + k, qb.at[me], sib).wait_send()
        copy(OO + k, osend.at[k], orecv.at[k], {"ctx": sib}).wait_send()
        copy(OS + k, ssend.at[k], srecv.at[k], {"ctx": sib}).wait_send()
    for k in range(7):
        copy(PW + k, pwsend, pwrecv.at[dp], {"ctx": sib}).wait_send()
    for n in range(4):
        copy(RL + n, relay.at[n], relay.at[n], {"ctx": sib}).wait_send()
        copy(RF + n, relay.at[n], relay.at[n], {"ctx": sib}).wait_send()
    for n in range(5):
        copy(PD + n, psend.at[0], precv.at[dp], {"ctx": sib}).wait_send()


def local(
    queries, keys, values, old_keys, old_values, conv_keys, conv_values, out_proj, residual, gain,
    span_order, memory_length,
):
    vm = pl.BlockSpec(memory_space=pltpu.VMEM)
    sm = pl.BlockSpec(memory_space=pltpu.SMEM)
    return pl.pallas_call(
        kernel,
        out_shape=jax.ShapeDtypeStruct(residual.shape, BF16),
        in_specs=[vm] * 10 + [sm] * 2,
        out_specs=vm,
        scratch_shapes=[
            pltpu.VMEM((16, 4, 144, 128), BF16),
            pltpu.VMEM((4, 144, 256), BF16),
            pltpu.VMEM((2, 16, 2, 64, 256), BF16),
            pltpu.VMEM((256, 512), F32),
            pltpu.VMEM((8, 512), F32),
            pltpu.VMEM((3, 256, 128), BF16),
            pltpu.VMEM((3, 256, 128), BF16),
            pltpu.VMEM((3, 8, 128), F32),
            pltpu.VMEM((4, 8, 128), F32),
            pltpu.VMEM((8, 128, 512), BF16),
            pltpu.VMEM((8, 128, 512), BF16),
            pltpu.VMEM((4, 64, 512), BF16),
            pltpu.VMEM((8, 128), F32),
            pltpu.VMEM((8, 8, 128), F32),
            pltpu.VMEM((128, 256), BF16),
            pltpu.VMEM((128, 512), F32),
            pltpu.SemaphoreType.DMA((COUNT,)),
            pltpu.SemaphoreType.DMA((COUNT,)),
        ],
        compiler_params=pltpu.CompilerParams(collective_id=0, has_side_effects=True),
    )(
        queries, keys, values, old_keys, old_values, conv_keys, conv_values, out_proj, residual,
        gain.reshape(1, -1), span_order, memory_length,
    )


def solution(mesh):
    placed = (
        P("ctx", "dp"),
        P("ctx", "dp"),
        P("ctx", "dp"),
        P("ctx", "dp"),
        P("ctx", "dp"),
        P("dp", None, None, None),
        P("dp", None, None, None),
        P("ctx", "dp"),
        P("ctx", "dp"),
        P("dp"),
        P("ctx"),
        P(),
    )
    return jax.shard_map(
        local, mesh=mesh, in_specs=placed, out_specs=P("ctx", "dp"), check_vma=False
    )
```

```python
import math

import jax
import jax.numpy as jnp
from jax import lax
from jax.experimental import pallas as pl
from jax.experimental.pallas import tpu as pltpu
from jax.sharding import PartitionSpec as P

MESH = pl.DeviceIdType.MESH
NEG = -1e30
HID = 1e9
F32 = jnp.float32
BF16 = jnp.bfloat16

KU, KD, WU, WD, SU, SD, SX, QQ, WY = 0, 32, 64, 72, 80, 88, 96, 98, 101
OO, OS, PW, RL, RF, PD, COUNT = 102, 105, 108, 115, 119, 123, 128


def dot(a, b, ca, cb):
    return lax.dot_general(a, b, (((ca,), (cb,)), ((), ())), preferred_element_type=F32)


def kernel(
    q_in, k_in, v_in, ok_in, ov_in, ck_in, cv_in, w_in, res_in, gain_in, span_in, mlen_in,
    out_ref,
    kv, qb, wall, acc, rows, osend, orecv, ssend, srecv, psend, precv, relay, pwsend, pwrecv, attn_s, stream_s,
    ssem, rsem,
):
    ctx = lax.axis_index("ctx")
    dp = lax.axis_index("dp")
    core = lax.rem(ctx, 2)
    z = lax.rem(lax.div(ctx, 2), 16)
    y = lax.div(ctx, 32)
    me = y * 2 + core

    def at(fy, fz, fc):
        return (fy * 16 + fz) * 2 + fc

    def behind(s):
        return lax.rem(z + 16 - s, 16)

    def ahead(s):
        return lax.rem(z + s, 16)

    up, down = at(y, ahead(1), core), at(y, behind(1), core)
    sib, other, cross = at(y, z, 1 - core), at(1 - y, z, core), at(1 - y, z, 1 - core)

    barrier = pltpu.get_barrier_semaphore()
    for peer in (up, down, sib, other, cross):
        pl.semaphore_signal(barrier, inc=1, device_id={"ctx": peer}, device_id_type=MESH)
    for k in range(1, 8):
        pl.semaphore_signal(barrier, inc=1, device_id={"dp": lax.rem(dp + k, 8)}, device_id_type=MESH)

    row16 = lax.broadcasted_iota(jnp.int32, (16, 256), 0)
    s0 = span_in[0].astype(F32)
    s1 = span_in[1].astype(F32)
    pick_r = lax.broadcasted_iota(jnp.int32, (16, 32), 0)
    pick_c = lax.broadcasted_iota(jnp.int32, (16, 32), 1)
    for half, (new, old, conv) in enumerate(((k_in, ok_in, ck_in), (v_in, ov_in, cv_in))):
        for h in range(2):
            kv[z, half * 2 + h, 0:128, :] = new[:, h * 128 : (h + 1) * 128]
        taps = []
        for t in range(4):
            pick = jnp.where(pick_c == pick_r * 4 + t, 1.0, 0.0).astype(BF16)
            taps.append(dot(pick, old[...], 1, 0).astype(BF16))
        heads = []
        for h in range(2):
            total = jnp.zeros((16, 128), F32)
            for t in range(4):
                total = total + dot(taps[t][:, h * 128 : (h + 1) * 128], conv[h, t], 1, 0)
            heads.append(total)
        mem = jnp.concatenate(heads, axis=1)
        if half == 0:
            mem = jnp.where(row16 == 8, s0, jnp.where(row16 == 9, s1, mem))
        for h in range(2):
            kv[z, half * 2 + h, 128:144, :] = mem[:, h * 128 : (h + 1) * 128].astype(BF16)
    qb[me, 0:128, :] = q_in[...]
    qb[me, 128:144, :] = jnp.where(row16 == 0, s0, jnp.where(row16 == 1, s1, 0.0)).astype(BF16)
    wall[y, z, core] = w_in[...]
    acc[...] = jnp.zeros_like(acc)
    rows[...] = jnp.where(lax.broadcasted_iota(jnp.int32, (8, 512), 0) < 2, NEG, 0.0)

    pl.semaphore_wait(barrier, 12)

    def copy(number, ref, dst, where):
        return pltpu.make_async_remote_copy(
            src_ref=ref, dst_ref=dst, send_sem=ssem.at[number], recv_sem=rsem.at[number],
            device_id=where, device_id_type=MESH,
        )

    def same(number, ref, where):
        return copy(number, ref, ref, {"ctx": where})

    def w_of(fz, c):
        return wall.at[:, fz, c]

    same(WY, wall.at[y, z, core], other).start()
    for c in (0, 1):
        same(KU + c * 8, kv.at[z, c], up).start()
        same(KD + c * 8, kv.at[z, c], down).start()
    for k, peer in enumerate((other, cross, sib)):
        same(QQ + k, qb.at[me], peer).start()
    for c in (2, 3):
        same(KU + c * 8, kv.at[z, c], up).start()
        same(KD + c * 8, kv.at[z, c], down).start()
    factor = math.log2(math.e) / math.sqrt(128.0)
    r = lax.broadcasted_iota(jnp.int32, (144, 128), 0)
    rf = r.astype(F32)
    first = (512 - mlen_in[0]).astype(F32)
    lane = lax.broadcasted_iota(jnp.int32, (8, 128), 1)

    def positions(fz):
        tail = kv[fz, 0, 128:144, :].astype(F32)
        slot = rf - 128.0 + (at(y, fz, core) * 8).astype(F32)
        mem_pos = jnp.where((slot >= first) & (r < 136), -1.0, HID)
        low = jnp.broadcast_to(tail[8:9] * 64.0, (144, 128)) + rf
        high = jnp.broadcast_to(tail[9:10] * 64.0 - 64.0, (144, 128)) + rf
        place = jnp.where(r < 64, low, jnp.where(r < 128, high, mem_pos))
        return jnp.concatenate([place] * 4, axis=1)

    def fold(blocks):
        parts = []
        for m in range(4):
            tail = qb[m, 128:144, 0:128].astype(F32)
            q0 = jnp.broadcast_to(tail[0:1], (8, 128))
            q1 = jnp.broadcast_to(tail[1:2], (8, 128))
            parts.append(jnp.where(lane < 64, q0 * 64.0, q1 * 64.0 - 64.0) + lane.astype(F32))
        qpos = jnp.concatenate(parts, axis=1)[0:1]
        vis = jnp.concatenate([positions(b) for b in blocks], axis=0) <= qpos
        for h in range(2):
            cols = slice(h * 128, (h + 1) * 128)
            keys = jnp.concatenate([kv[b, h] for b in blocks], axis=0)
            vals = jnp.concatenate([kv[b, 2 + h] for b in blocks], axis=0)
            s = dot(keys, qb[:, 0:128, cols].reshape(512, 128), 1, 1) * factor
            s = jnp.where(vis, s, NEG)
            before = rows[h : h + 1, :]
            top = jnp.maximum(before, jnp.max(s, axis=0, keepdims=True))
            p = jnp.where(vis, jnp.exp2(s - top), 0.0)
            shrink = jnp.exp2(before - top)
            rows[h : h + 1, :] = top
            rows[h + 2 : h + 3, :] = rows[h + 2 : h + 3, :] * shrink + jnp.sum(p, axis=0, keepdims=True)
            acc[cols, :] = acc[cols, :] * shrink + dot(vals, p.astype(BF16), 0, 0)

    def ring(s):
        for c in range(4):
            for base, at_z, to in ((KU + c * 8, behind(s), up), (KD + c * 8, ahead(s), down)):
                same(base + s - 1, kv.at[at_z, c], to).wait_recv()
                same(base + s, kv.at[at_z, c], to).start()

    def ring_w(s):
        for base, side, at_z, to in ((WU, SU, behind(s), up), (WD, SD, ahead(s), down)):
            same(base + s - 1, w_of(at_z, core), to).wait_recv()
            same(base + s, w_of(at_z, core), to).start()
            same(side + s - 1, w_of(at_z, core), sib).start()

    ring(1)
    same(WY, wall.at[1 - y, z, core], other).wait_recv()
    same(WU, w_of(z, core), up).start()
    same(WD, w_of(z, core), down).start()
    same(SX, w_of(z, core), sib).start()
    for k, (fy, fc) in enumerate(((1 - y, core), (1 - y, 1 - core), (y, 1 - core))):
        same(QQ + k, qb.at[fy * 2 + fc], other).wait_recv()

    def stage(s, carry):
        fold([behind(s), ahead(s)])
        ring(s + 1)
        ring_w(s)
        return carry

    lax.fori_loop(1, 6, stage, 0)
    fold([behind(6), ahead(6)])
    lo, hi, far = behind(7), ahead(7), ahead(8)
    for c in range(4):
        for base, at_z, to in ((KU + c * 8, lo, up), (KD + c * 8, hi, down)):
            same(base + 6, kv.at[at_z, c], to).wait_recv()
            if (to is up) == (c % 2 == 0):
                same(base + 7, kv.at[at_z, c], to).start()
    ring_w(6)
    fold([lo, hi])
    for base, side, at_z, to, fy in ((WU, SU, lo, up, 0), (WD, SD, hi, down, 1)):
        same(base + 6, w_of(at_z, core), to).wait_recv()
        same(base + 7, wall.at[fy, at_z, core], to).start()
        same(side + 6, w_of(at_z, core), sib).start()
    for c in range(4):
        same((KD if c % 2 else KU) + c * 8 + 7, kv.at[far, c], up).wait_recv()
    fold([far, z])

    for k, (fy, fc) in enumerate(((1 - y, core), (1 - y, 1 - core), (y, 1 - core))):
        m = fy * 2 + fc
        peer = (other, cross, sib)[k]
        lanes = pl.ds(pl.multiple_of(m * 128, 128), 128)
        osend[k] = acc[:, lanes].astype(BF16)
        ssend[k] = rows[:, lanes]
        copy(OO + k, osend.at[k], orecv.at[k], {"ctx": peer}).start()
        copy(OS + k, ssend.at[k], srecv.at[k], {"ctx": peer}).start()
    lanes = pl.ds(pl.multiple_of(me * 128, 128), 128)
    srecv[3] = rows[:, lanes]

    for base, fy in ((WU, 0), (WD, 1)):
        same(base + 7, wall.at[fy, far, core], up).wait_recv()
    same(SX + 1, w_of(far, core), sib).start()

    for k in range(3):
        copy(OO + k, osend.at[k], orecv.at[k], {"ctx": sib}).wait_recv()
        copy(OS + k, ssend.at[k], srecv.at[k], {"ctx": sib}).wait_recv()
    for h in range(2):
        cols = slice(h * 128, (h + 1) * 128)
        tops = srecv[:, h, :]
        sums = srecv[:, h + 2, :]
        best = jnp.max(tops, axis=0, keepdims=True)
        weight = jnp.exp2(tops - best)
        total = jnp.sum(weight * sums, axis=0, keepdims=True)
        mixed = acc[cols, lanes] * weight[3:4]
        for j in range(3):
            mixed = mixed + orecv[j, cols, :].astype(F32) * weight[j : j + 1]
        attn_s[:, cols] = (mixed / total).T.astype(BF16)

    for s in range(1, 8):
        same(SU + s - 1, w_of(behind(s), 1 - core), sib).wait_recv()
        same(SD + s - 1, w_of(ahead(s), 1 - core), sib).wait_recv()
    same(SX, w_of(z, 1 - core), sib).wait_recv()
    same(SX + 1, w_of(far, 1 - core), sib).wait_recv()

    def project(g):
        block = wall[lax.div(g, 4), pl.ds(lax.rem(g, 4) * 4, 4)]
        return dot(attn_s[...], block.reshape(512, 256), 1, 1)

    px = lax.div(dp, 2)
    py = lax.rem(dp, 2)

    def dp_at(dx, flip):
        return lax.rem(px + 4 + dx, 4) * 2 + (1 - py if flip else py)

    for flip in (0, 1):
        g = dp_at(2, flip)
        psend[g] = project(g).astype(BF16)
        for way, dx in ((0, 1), (1, -1)):
            copy(RL + way * 2 + flip, psend.at[g, pl.ds(way * 64, 64)], relay.at[way * 2 + flip], {"dp": dp_at(dx, flip)}).start()
    straight = ((1, 0), (-1, 0), (1, 1), (-1, 1), (0, 1))
    for n, (dx, flip) in enumerate(straight):
        g = dp_at(dx, flip)
        psend[g] = project(g).astype(BF16)
        copy(PD + n, psend.at[g], precv.at[dp], {"dp": g}).start()
    for flip in (0, 1):
        for way, dx in ((0, 1), (1, -1)):
            n = way * 2 + flip
            copy(RL + n, relay.at[n], relay.at[n], {"dp": dp_at(dx, 0)}).wait_recv()
            copy(RF + n, relay.at[n], precv.at[dp_at(-dx, flip), pl.ds(way * 64, 64)], {"dp": dp_at(dx, 0)}).start()
    stream_s[...] = res_in[...].astype(F32) + project(dp)
    for n, (dx, flip) in enumerate(straight):
        src = dp_at(-dx, flip)
        copy(PD + n, psend.at[src], precv.at[src], {"dp": dp_at(1, 0)}).wait_recv()
        stream_s[...] += precv[src].astype(F32)
    for flip in (0, 1):
        src = dp_at(2, flip)
        for way in (0, 1):
            n = way * 2 + flip
            copy(RF + n, relay.at[n], precv.at[src, pl.ds(way * 64, 64)], {"dp": dp_at(1, 0)}).wait_recv()
        stream_s[...] += precv[src].astype(F32)

    stream = stream_s[...]
    mine = jnp.sum(stream * stream, axis=1, keepdims=True)
    line = jnp.broadcast_to(mine, (128, 128)).T
    pwsend[...] = line[0:8]
    pwrecv[dp] = line[0:8]
    for k in range(1, 8):
        copy(PW + k - 1, pwsend, pwrecv.at[dp], {"dp": lax.rem(dp + k, 8)}).start()
    for k in range(1, 8):
        src = lax.rem(dp + 8 - k, 8)
        copy(PW + k - 1, pwsend, pwrecv.at[src], {"dp": src}).wait_recv()
    power = jnp.sum(pwrecv[...], axis=0)[0:1] / 4096.0
    norm = jnp.broadcast_to(lax.rsqrt(power + 1e-6), (128, 128)).T
    for c in range(4):
        cols = slice(c * 128, (c + 1) * 128)
        out_ref[:, cols] = (stream_s[:, cols] * norm * gain_in[cols].astype(F32).reshape(1, 128)).astype(BF16)

    for s in range(8):
        for c in range(4):
            for base in (KU, KD):
                if s < 7 or (base == KU) == (c % 2 == 0):
                    same(base + c * 8 + s, kv.at[z, c], up).wait_send()
        if s < 7:
            same(SU + s, w_of(z, core), sib).wait_send()
            same(SD + s, w_of(z, core), sib).wait_send()
        for base in (WU, WD):
            same(base + s, w_of(z, core) if s < 7 else wall.at[0, z, core], up).wait_send()
    same(SX, w_of(z, core), sib).wait_send()
    same(SX + 1, w_of(z, core), sib).wait_send()
    same(WY, wall.at[y, z, core], other).wait_send()
    for k in range(3):
        same(QQ + k, qb.at[me], sib).wait_send()
        copy(OO + k, osend.at[k], orecv.at[k], {"ctx": sib}).wait_send()
        copy(OS + k, ssend.at[k], srecv.at[k], {"ctx": sib}).wait_send()
    for k in range(7):
        copy(PW + k, pwsend, pwrecv.at[dp], {"ctx": sib}).wait_send()
    for n in range(4):
        copy(RL + n, relay.at[n], relay.at[n], {"ctx": sib}).wait_send()
        copy(RF + n, relay.at[n], relay.at[n], {"ctx": sib}).wait_send()
    for n in range(5):
        copy(PD + n, psend.at[0], precv.at[dp], {"ctx": sib}).wait_send()


def local(
    queries, keys, values, old_keys, old_values, conv_keys, conv_values, out_proj, residual, gain,
    span_order, memory_length,
):
    vm = pl.BlockSpec(memory_space=pltpu.VMEM)
    sm = pl.BlockSpec(memory_space=pltpu.SMEM)
    return pl.pallas_call(
        kernel,
        out_shape=jax.ShapeDtypeStruct(residual.shape, BF16),
        in_specs=[vm] * 10 + [sm] * 2,
        out_specs=vm,
        scratch_shapes=[
            pltpu.VMEM((16, 4, 144, 128), BF16),
            pltpu.VMEM((4, 144, 256), BF16),
            pltpu.VMEM((2, 16, 2, 64, 256), BF16),
            pltpu.VMEM((256, 512), F32),
            pltpu.VMEM((8, 512), F32),
            pltpu.VMEM((3, 256, 128), BF16),
            pltpu.VMEM((3, 256, 128), BF16),
            pltpu.VMEM((3, 8, 128), F32),
            pltpu.VMEM((4, 8, 128), F32),
            pltpu.VMEM((8, 128, 512), BF16),
            pltpu.VMEM((8, 128, 512), BF16),
            pltpu.VMEM((4, 64, 512), BF16),
            pltpu.VMEM((8, 128), F32),
            pltpu.VMEM((8, 8, 128), F32),
            pltpu.VMEM((128, 256), BF16),
            pltpu.VMEM((128, 512), F32),
            pltpu.SemaphoreType.DMA((COUNT,)),
            pltpu.SemaphoreType.DMA((COUNT,)),
        ],
        compiler_params=pltpu.CompilerParams(collective_id=0, has_side_effects=True),
    )(
        queries, keys, values, old_keys, old_values, conv_keys, conv_values, out_proj, residual,
        gain, span_order, memory_length,
    )


def solution(mesh):
    placed = (
        P("ctx", "dp"),
        P("ctx", "dp"),
        P("ctx", "dp"),
        P("ctx", "dp"),
        P("ctx", "dp"),
        P("dp", None, None, None),
        P("dp", None, None, None),
        P("ctx", "dp"),
        P("ctx", "dp"),
        P("dp"),
        P("ctx"),
        P(),
    )
    return jax.shard_map(
        local, mesh=mesh, in_specs=placed, out_specs=P("ctx", "dp"), check_vma=False
    )
```

```python
import math

import jax
import jax.numpy as jnp
from jax import lax
from jax.experimental import pallas as pl
from jax.experimental.pallas import tpu as pltpu
from jax.sharding import PartitionSpec as P

MESH = pl.DeviceIdType.MESH
NEG = -1e30
HID = 1e9
F32 = jnp.float32
BF16 = jnp.bfloat16

KU, KD, WU, WD, SU, SD, SX, QQ, WY = 0, 32, 64, 72, 80, 88, 96, 98, 101
OO, OS, PW, RL, RF, PD, COUNT = 102, 105, 108, 115, 119, 123, 128


def dot(a, b, ca, cb):
    return lax.dot_general(a, b, (((ca,), (cb,)), ((), ())), preferred_element_type=F32)


def kernel(
    q_in, k_in, v_in, ok_in, ov_in, ck_in, cv_in, w_in, res_in, gain_in, span_in, mlen_in,
    out_ref,
    kv, qb, wall, acc, rows, osend, orecv, ssend, srecv, psend, precv, relay, pwsend, pwrecv, attn_s, stream_s,
    ssem, rsem,
):
    ctx = lax.axis_index("ctx")
    dp = lax.axis_index("dp")
    core = lax.rem(ctx, 2)
    z = lax.rem(lax.div(ctx, 2), 16)
    y = lax.div(ctx, 32)
    me = y * 2 + core

    def at(fy, fz, fc):
        return (fy * 16 + fz) * 2 + fc

    def behind(s):
        return lax.rem(z + 16 - s, 16)

    def ahead(s):
        return lax.rem(z + s, 16)

    up, down = at(y, ahead(1), core), at(y, behind(1), core)
    sib, other, cross = at(y, z, 1 - core), at(1 - y, z, core), at(1 - y, z, 1 - core)

    barrier = pltpu.get_barrier_semaphore()
    for peer in (up, down, sib, other, cross):
        pl.semaphore_signal(barrier, inc=1, device_id={"ctx": peer}, device_id_type=MESH)
    for k in range(1, 8):
        pl.semaphore_signal(barrier, inc=1, device_id={"dp": lax.rem(dp + k, 8)}, device_id_type=MESH)

    row16 = lax.broadcasted_iota(jnp.int32, (16, 256), 0)
    s0 = span_in[0].astype(F32)
    s1 = span_in[1].astype(F32)
    pick_r = lax.broadcasted_iota(jnp.int32, (16, 32), 0)
    pick_c = lax.broadcasted_iota(jnp.int32, (16, 32), 1)
    for half, (new, old, conv) in enumerate(((k_in, ok_in, ck_in), (v_in, ov_in, cv_in))):
        for h in range(2):
            kv[z, half * 2 + h, 0:128, :] = new[:, h * 128 : (h + 1) * 128]
        taps = []
        for t in range(4):
            pick = jnp.where(pick_c == pick_r * 4 + t, 1.0, 0.0).astype(BF16)
            taps.append(dot(pick, old[...], 1, 0).astype(BF16))
        heads = []
        for h in range(2):
            total = jnp.zeros((16, 128), F32)
            for t in range(4):
                total = total + dot(taps[t][:, h * 128 : (h + 1) * 128], conv[h, t], 1, 0)
            heads.append(total)
        mem = jnp.concatenate(heads, axis=1)
        if half == 0:
            mem = jnp.where(row16 == 8, s0, jnp.where(row16 == 9, s1, mem))
        for h in range(2):
            kv[z, half * 2 + h, 128:144, :] = mem[:, h * 128 : (h + 1) * 128].astype(BF16)
    qb[me, 0:128, :] = q_in[...]
    qb[me, 128:144, :] = jnp.where(row16 == 0, s0, jnp.where(row16 == 1, s1, 0.0)).astype(BF16)
    wall[y, z, core] = w_in[...]
    acc[...] = jnp.zeros_like(acc)
    rows[...] = jnp.where(lax.broadcasted_iota(jnp.int32, (8, 512), 0) < 2, NEG, 0.0)

    pl.semaphore_wait(barrier, 12)

    def copy(number, ref, dst, where):
        return pltpu.make_async_remote_copy(
            src_ref=ref, dst_ref=dst, send_sem=ssem.at[number], recv_sem=rsem.at[number],
            device_id=where, device_id_type=MESH,
        )

    def same(number, ref, where):
        return copy(number, ref, ref, {"ctx": where})

    def w_of(fz, c):
        return wall.at[:, fz, c]

    same(WY, wall.at[y, z, core], other).start()
    for c in (0, 1):
        same(KU + c * 8, kv.at[z, c], up).start()
        same(KD + c * 8, kv.at[z, c], down).start()
    for k, peer in enumerate((other, cross, sib)):
        same(QQ + k, qb.at[me], peer).start()
    for c in (2, 3):
        same(KU + c * 8, kv.at[z, c], up).start()
        same(KD + c * 8, kv.at[z, c], down).start()
    factor = math.log2(math.e) / math.sqrt(128.0)
    r = lax.broadcasted_iota(jnp.int32, (144, 128), 0)
    rf = r.astype(F32)
    first = (512 - mlen_in[0]).astype(F32)
    lane = lax.broadcasted_iota(jnp.int32, (8, 128), 1)

    def positions(fz):
        tail = kv[fz, 0, 128:144, :].astype(F32)
        slot = rf - 128.0 + (at(y, fz, core) * 8).astype(F32)
        mem_pos = jnp.where((slot >= first) & (r < 136), -1.0, HID)
        low = jnp.broadcast_to(tail[8:9] * 64.0, (144, 128)) + rf
        high = jnp.broadcast_to(tail[9:10] * 64.0 - 64.0, (144, 128)) + rf
        place = jnp.where(r < 64, low, jnp.where(r < 128, high, mem_pos))
        return jnp.concatenate([place] * 4, axis=1)

    def fold(blocks):
        parts = []
        for m in range(4):
            tail = qb[m, 128:144, 0:128].astype(F32)
            q0 = jnp.broadcast_to(tail[0:1], (8, 128))
            q1 = jnp.broadcast_to(tail[1:2], (8, 128))
            parts.append(jnp.where(lane < 64, q0 * 64.0, q1 * 64.0 - 64.0) + lane.astype(F32))
        qpos = jnp.concatenate(parts, axis=1)[0:1]
        vis = jnp.concatenate([positions(b) for b in blocks], axis=0) <= qpos
        for h in range(2):
            cols = slice(h * 128, (h + 1) * 128)
            keys = jnp.concatenate([kv[b, h] for b in blocks], axis=0)
            vals = jnp.concatenate([kv[b, 2 + h] for b in blocks], axis=0)
            s = dot(keys, qb[:, 0:128, cols].reshape(512, 128), 1, 1) * factor
            s = jnp.where(vis, s, NEG)
            before = rows[h : h + 1, :]
            top = jnp.maximum(before, jnp.max(s, axis=0, keepdims=True))
            p = jnp.where(vis, jnp.exp2(s - top), 0.0)
            shrink = jnp.exp2(before - top)
            rows[h : h + 1, :] = top
            rows[h + 2 : h + 3, :] = rows[h + 2 : h + 3, :] * shrink + jnp.sum(p, axis=0, keepdims=True)
            acc[cols, :] = acc[cols, :] * shrink + dot(vals, p.astype(BF16), 0, 0)

    def ring(s):
        for c in range(4):
            for base, at_z, to in ((KU + c * 8, behind(s), up), (KD + c * 8, ahead(s), down)):
                same(base + s - 1, kv.at[at_z, c], to).wait_recv()
                same(base + s, kv.at[at_z, c], to).start()

    def ring_w(s):
        for base, side, at_z, to in ((WU, SU, behind(s), up), (WD, SD, ahead(s), down)):
            same(base + s - 1, w_of(at_z, core), to).wait_recv()
            same(base + s, w_of(at_z, core), to).start()
            same(side + s - 1, w_of(at_z, core), sib).start()

    ring(1)
    same(WY, wall.at[1 - y, z, core], other).wait_recv()
    same(WU, w_of(z, core), up).start()
    same(WD, w_of(z, core), down).start()
    same(SX, w_of(z, core), sib).start()
    for k, (fy, fc) in enumerate(((1 - y, core), (1 - y, 1 - core), (y, 1 - core))):
        same(QQ + k, qb.at[fy * 2 + fc], other).wait_recv()

    def stage(s, carry):
        fold([behind(s), ahead(s)])
        ring(s + 1)
        ring_w(s)
        return carry

    lax.fori_loop(1, 6, stage, 0)
    fold([behind(6), ahead(6)])
    lo, hi, far = behind(7), ahead(7), ahead(8)
    for c in range(4):
        for base, at_z, to in ((KU + c * 8, lo, up), (KD + c * 8, hi, down)):
            same(base + 6, kv.at[at_z, c], to).wait_recv()
            if (to is up) == (c % 2 == 0):
                same(base + 7, kv.at[at_z, c], to).start()
    ring_w(6)
    fold([lo, hi])
    for base, side, at_z, to, fy in ((WU, SU, lo, up, 0), (WD, SD, hi, down, 1)):
        same(base + 6, w_of(at_z, core), to).wait_recv()
        same(base + 7, wall.at[fy, at_z, core], to).start()
        same(side + 6, w_of(at_z, core), sib).start()
    fold([z])
    for c in range(4):
        same((KD if c % 2 else KU) + c * 8 + 7, kv.at[far, c], up).wait_recv()
    fold([far])

    for k, (fy, fc) in enumerate(((1 - y, core), (1 - y, 1 - core), (y, 1 - core))):
        m = fy * 2 + fc
        peer = (other, cross, sib)[k]
        lanes = pl.ds(pl.multiple_of(m * 128, 128), 128)
        osend[k] = acc[:, lanes].astype(BF16)
        ssend[k] = rows[:, lanes]
        copy(OO + k, osend.at[k], orecv.at[k], {"ctx": peer}).start()
        copy(OS + k, ssend.at[k], srecv.at[k], {"ctx": peer}).start()
    lanes = pl.ds(pl.multiple_of(me * 128, 128), 128)
    srecv[3] = rows[:, lanes]

    for base, fy in ((WU, 0), (WD, 1)):
        same(base + 7, wall.at[fy, far, core], up).wait_recv()
    same(SX + 1, w_of(far, core), sib).start()

    for k in range(3):
        copy(OO + k, osend.at[k], orecv.at[k], {"ctx": sib}).wait_recv()
        copy(OS + k, ssend.at[k], srecv.at[k], {"ctx": sib}).wait_recv()
    for h in range(2):
        cols = slice(h * 128, (h + 1) * 128)
        tops = srecv[:, h, :]
        sums = srecv[:, h + 2, :]
        best = jnp.max(tops, axis=0, keepdims=True)
        weight = jnp.exp2(tops - best)
        total = jnp.sum(weight * sums, axis=0, keepdims=True)
        mixed = acc[cols, lanes] * weight[3:4]
        for j in range(3):
            mixed = mixed + orecv[j, cols, :].astype(F32) * weight[j : j + 1]
        attn_s[:, cols] = (mixed / total).T.astype(BF16)

    for s in range(1, 8):
        same(SU + s - 1, w_of(behind(s), 1 - core), sib).wait_recv()
        same(SD + s - 1, w_of(ahead(s), 1 - core), sib).wait_recv()
    same(SX, w_of(z, 1 - core), sib).wait_recv()
    same(SX + 1, w_of(far, 1 - core), sib).wait_recv()

    def project(g):
        block = wall[lax.div(g, 4), pl.ds(lax.rem(g, 4) * 4, 4)]
        return dot(attn_s[...], block.reshape(512, 256), 1, 1)

    px = lax.div(dp, 2)
    py = lax.rem(dp, 2)

    def dp_at(dx, flip):
        return lax.rem(px + 4 + dx, 4) * 2 + (1 - py if flip else py)

    for flip in (0, 1):
        g = dp_at(2, flip)
        psend[g] = project(g).astype(BF16)
        for way, dx in ((0, 1), (1, -1)):
            copy(RL + way * 2 + flip, psend.at[g, pl.ds(way * 64, 64)], relay.at[way * 2 + flip], {"dp": dp_at(dx, flip)}).start()
    straight = ((1, 0), (-1, 0), (1, 1), (-1, 1), (0, 1))
    for n, (dx, flip) in enumerate(straight):
        g = dp_at(dx, flip)
        psend[g] = project(g).astype(BF16)
        copy(PD + n, psend.at[g], precv.at[dp], {"dp": g}).start()
    for flip in (0, 1):
        for way, dx in ((0, 1), (1, -1)):
            n = way * 2 + flip
            copy(RL + n, relay.at[n], relay.at[n], {"dp": dp_at(dx, 0)}).wait_recv()
            copy(RF + n, relay.at[n], precv.at[dp_at(-dx, flip), pl.ds(way * 64, 64)], {"dp": dp_at(dx, 0)}).start()
    stream_s[...] = res_in[...].astype(F32) + project(dp)
    for n, (dx, flip) in enumerate(straight):
        src = dp_at(-dx, flip)
        copy(PD + n, psend.at[src], precv.at[src], {"dp": dp_at(1, 0)}).wait_recv()
        stream_s[...] += precv[src].astype(F32)
    for flip in (0, 1):
        src = dp_at(2, flip)
        for way in (0, 1):
            n = way * 2 + flip
            copy(RF + n, relay.at[n], precv.at[src, pl.ds(way * 64, 64)], {"dp": dp_at(1, 0)}).wait_recv()
        stream_s[...] += precv[src].astype(F32)

    stream = stream_s[...]
    mine = jnp.sum(stream * stream, axis=1, keepdims=True)
    line = jnp.broadcast_to(mine, (128, 128)).T
    pwsend[...] = line[0:8]
    pwrecv[dp] = line[0:8]
    for k in range(1, 8):
        copy(PW + k - 1, pwsend, pwrecv.at[dp], {"dp": lax.rem(dp + k, 8)}).start()
    for k in range(1, 8):
        src = lax.rem(dp + 8 - k, 8)
        copy(PW + k - 1, pwsend, pwrecv.at[src], {"dp": src}).wait_recv()
    power = jnp.sum(pwrecv[...], axis=0)[0:1] / 4096.0
    norm = jnp.broadcast_to(lax.rsqrt(power + 1e-6), (128, 128)).T
    for c in range(4):
        cols = slice(c * 128, (c + 1) * 128)
        out_ref[:, cols] = (stream_s[:, cols] * norm * gain_in[cols].astype(F32).reshape(1, 128)).astype(BF16)

    for s in range(8):
        for c in range(4):
            for base in (KU, KD):
                if s < 7 or (base == KU) == (c % 2 == 0):
                    same(base + c * 8 + s, kv.at[z, c], up).wait_send()
        if s < 7:
            same(SU + s, w_of(z, core), sib).wait_send()
            same(SD + s, w_of(z, core), sib).wait_send()
        for base in (WU, WD):
            same(base + s, w_of(z, core) if s < 7 else wall.at[0, z, core], up).wait_send()
    same(SX, w_of(z, core), sib).wait_send()
    same(SX + 1, w_of(z, core), sib).wait_send()
    same(WY, wall.at[y, z, core], other).wait_send()
    for k in range(3):
        same(QQ + k, qb.at[me], sib).wait_send()
        copy(OO + k, osend.at[k], orecv.at[k], {"ctx": sib}).wait_send()
        copy(OS + k, ssend.at[k], srecv.at[k], {"ctx": sib}).wait_send()
    for k in range(7):
        copy(PW + k, pwsend, pwrecv.at[dp], {"ctx": sib}).wait_send()
    for n in range(4):
        copy(RL + n, relay.at[n], relay.at[n], {"ctx": sib}).wait_send()
        copy(RF + n, relay.at[n], relay.at[n], {"ctx": sib}).wait_send()
    for n in range(5):
        copy(PD + n, psend.at[0], precv.at[dp], {"ctx": sib}).wait_send()


def local(
    queries, keys, values, old_keys, old_values, conv_keys, conv_values, out_proj, residual, gain,
    span_order, memory_length,
):
    vm = pl.BlockSpec(memory_space=pltpu.VMEM)
    sm = pl.BlockSpec(memory_space=pltpu.SMEM)
    return pl.pallas_call(
        kernel,
        out_shape=jax.ShapeDtypeStruct(residual.shape, BF16),
        in_specs=[vm] * 10 + [sm] * 2,
        out_specs=vm,
        scratch_shapes=[
            pltpu.VMEM((16, 4, 144, 128), BF16),
            pltpu.VMEM((4, 144, 256), BF16),
            pltpu.VMEM((2, 16, 2, 64, 256), BF16),
            pltpu.VMEM((256, 512), F32),
            pltpu.VMEM((8, 512), F32),
            pltpu.VMEM((3, 256, 128), BF16),
            pltpu.VMEM((3, 256, 128), BF16),
            pltpu.VMEM((3, 8, 128), F32),
            pltpu.VMEM((4, 8, 128), F32),
            pltpu.VMEM((8, 128, 512), BF16),
            pltpu.VMEM((8, 128, 512), BF16),
            pltpu.VMEM((4, 64, 512), BF16),
            pltpu.VMEM((8, 128), F32),
            pltpu.VMEM((8, 8, 128), F32),
            pltpu.VMEM((128, 256), BF16),
            pltpu.VMEM((128, 512), F32),
            pltpu.SemaphoreType.DMA((COUNT,)),
            pltpu.SemaphoreType.DMA((COUNT,)),
        ],
        compiler_params=pltpu.CompilerParams(collective_id=0, has_side_effects=True),
    )(
        queries, keys, values, old_keys, old_values, conv_keys, conv_values, out_proj, residual,
        gain, span_order, memory_length,
    )


def solution(mesh):
    placed = (
        P("ctx", "dp"),
        P("ctx", "dp"),
        P("ctx", "dp"),
        P("ctx", "dp"),
        P("ctx", "dp"),
        P("dp", None, None, None),
        P("dp", None, None, None),
        P("ctx", "dp"),
        P("ctx", "dp"),
        P("dp"),
        P("ctx"),
        P(),
    )
    return jax.shard_map(
        local, mesh=mesh, in_specs=placed, out_specs=P("ctx", "dp"), check_vma=False
    )
```
